128 devices in a mesh: post: 16 (over z, y), sub: 8 (over x, core).
Axes of the slice: x: 4, y: 4, z: 4, core: 2. Of those that a mesh axis runs over, the one named last changes fastest.
Arguments:
- vectors: bfloat16 [4096, 4096], P(('post', 'sub')), may hold values from -6 to 6
- owner_group_index: int32 [4096, 8], P(('post', 'sub')), may hold values from 0 to 15, all different within a row; in each aligned block of 32 rows (0 to 31, 32 to 63, ...) at most 24 rows name the same one
- local_posting_index: int32 [4096, 8], P(('post', 'sub')), may hold values from 0 to 8191
- slot_valid_mask: int32 [4096, 8], P(('post', 'sub')), may hold values 0 or 1
- slot_posting_weight: bfloat16 [4096, 8], P(('post', 'sub')), may hold values from 0.099609375 to 1
- centroids: bfloat16 [131072, 4096], P('post', 'sub'), may hold values from -4.1875 to 4.1875
- codebook: float32 [64, 256, 64], P('sub'), may hold values from -4.2 to 4.2
- variance: float32 [64], P('sub'), may hold values from 0.5 to 4
Outputs:
- trained_codebook: float32 [64, 256, 64], P('sub')
- slot_quant_error: float32 [4096, 8], P(('post', 'sub'))
The draws below stay inside these ranges and needn't reach their ends.
Inputs may be any that keep to these rules, and one draw needn't show every extreme that they name: `owner_group_index`: each row names 8 different owners. Within the rows of one device (aligned blocks of 32 rows) no owner is named by more than 24 slots, and in some blocks one owner is named by exactly 24.
All inputs are finite; a program needn't handle non-finite values. No bound on the sum of `slot_valid_mask` on one device may be relied on, other than what follows from the above.
Results may differ from the reference program's by a relative error of at most 0.0004.
Values may be sent and summed in bfloat16 or wider, within the bound.
No kernel may reach another device: no remote copies, remote signals or barrier semaphores. Data moves between devices by JAX's collectives and lax.ppermute only.
A program may use at most 128 MiB of HBM per device.

```python
import math
import jax
import jax.numpy as jnp
import numpy as np
from jax import lax

D = 4096
SUBS = 64
SD = 64
K = 256
P_SIZE = 131072
TOP = 8
ITERS = 2
ROWS_DEV = 32
ROWS = 4096
PDEV = 8192
CAPACITY = 24
N_POST = 16


def plant(array, key, least, largest):
    longest = array.shape.index(max(array.shape))
    spots = []
    for shift in (0, 1):
        where = [jax.random.randint(jax.random.fold_in(key, axis), (), 0, length) for axis, length in enumerate(array.shape)]
        where[longest] = (where[longest] + shift) % array.shape[longest]
        spots.append(tuple(where))
    return array.at[spots[0]].set(least).at[spots[1]].set(largest)


def shard_levels(rng, extent, shards, least, largest):
    factor_of, own = 1.0, jax.random.fold_in(rng, 6)
    for position, blocks in shards:
        draws = jnp.exp(jax.random.uniform(jax.random.fold_in(own, position), (blocks,), jnp.float32, least / len(shards), largest / len(shards)))
        factor_of = factor_of * jnp.repeat(draws, extent[position] // blocks).reshape([-1 if axis == position else 1 for axis in range(len(extent))])
    return factor_of


def routed_block(key, own, number, rows, count, top, bound, lean):
    ranking = jax.random.permutation(key, count)
    heavy_load, usual = portions_of(count, rows * top, bound, lean, True), portions_of(count, rows * top, bound, lean, False)
    places = jnp.arange(count)

    def named(lengths, offset_by):
        used = int((lengths > 0).sum())
        fixed = max(1, used // 4)
        shifted = fixed + (places - fixed + offset_by * (used - fixed)) % max(1, count - fixed)
        return jnp.zeros((count,), jnp.int32).at[ranking[jnp.where(places < fixed, places, shifted)]].set(jnp.asarray(lengths, jnp.int32))

    lengths = jnp.where(number % 4 == 0, named(heavy_load, number // 4), named(usual, number - number // 4 - 1))
    mixed = jax.random.permutation(jax.random.fold_in(own, 3), count)
    giver, sink = mixed[0:count // 2 * 2:2], mixed[1:count // 2 * 2:2]
    margin = jnp.minimum(lengths[giver] - 1, bound - lengths[sink]) // 2
    margin = jnp.where((giver == ranking[0]) | (sink == ranking[0]) | (lengths[sink] == 0), 0, jnp.maximum(margin, 0))
    shifted = jax.random.randint(jax.random.fold_in(own, 4), (count // 2,), 0, 1 << 20) % (margin + 1)
    lengths = lengths.at[giver].add(-shifted).at[sink].add(shifted)
    members = jnp.searchsorted(jnp.cumsum(lengths), jnp.arange(rows * top), side="right").astype(jnp.int32)
    grid = members.reshape(top, rows).T
    grid = grid[jax.random.permutation(jax.random.fold_in(own, 1), rows)]
    offset_by = jax.random.randint(jax.random.fold_in(own, 2), (rows, 1), 0, top)
    return jnp.take_along_axis(grid, (jnp.arange(top)[None, :] + offset_by) % top, axis=1)


def portions_of(count, total, limit, lean, full):
    portions = [(1 << 20) // math.isqrt(grade ** lean) + 1 for grade in range(1, count + 1)]
    largest = limit if full else min(limit, max(-(-total // count), total * portions[0] // sum(portions)))
    least = 1 if total - largest >= count - 1 else 0
    holding, rest = [largest] + [least] * (count - 1), total - largest - least * (count - 1)
    while rest > 0:
        free = [i for i in range(1, count) if holding[i] < largest] or [i for i in range(1, count) if holding[i] < limit]
        whole, remaining = sum([portions[i] for i in free]), rest
        for i in free:
            addition = min(limit - holding[i], max(1, remaining * portions[i] // whole), rest)
            holding[i] = holding[i] + addition
            rest = rest - addition
    return np.array(holding)


def noise(own_key, shape, deviation, reach, shards=(), held_as=jnp.bfloat16):
    array = jax.random.normal(own_key, shape, jnp.float32) * deviation
    if len(shards) > 0:
        array = shard_levels(own_key, shape, shards, -0.22, 0.18) * array
    return jnp.clip(array, min=-reach, max=reach).astype(held_as)


def setup_inputs(seed: int = 0) -> dict:
    key_list = jax.random.split(jax.random.key(seed), 9)
    vectors = noise(key_list[0], (ROWS, D), 1.0, 6.0, ((0, 128),))
    owner_group_index_keys = jax.random.split(jax.random.fold_in(key_list[1], 1), ROWS // ROWS_DEV)
    owner_group_index_turns = jax.random.permutation(jax.random.fold_in(key_list[1], 3), ROWS // ROWS_DEV)
    owner_group_index = jax.vmap(lambda own, number: routed_block(jax.random.fold_in(key_list[1], 2), own, number, ROWS_DEV, N_POST, TOP, CAPACITY, 2))(owner_group_index_keys, owner_group_index_turns).reshape((ROWS, TOP))
    local_posting_index = plant(jax.random.randint(key_list[2], (ROWS, TOP), 0, PDEV), jax.random.fold_in(key_list[2], 1), 0, PDEV - 1).astype(jnp.int32)
    slot_valid_mask = plant((jax.random.randint(key_list[3], (ROWS, TOP), 0, 4) < 3).astype(jnp.int32), jax.random.fold_in(key_list[3], 1), 0, 1)
    slot_posting_weight = jnp.clip(0.099609375 + 0.9003906 * jax.random.uniform(key_list[4], (ROWS, TOP), jnp.float32) ** shard_levels(key_list[4], (ROWS, TOP), ((0, 128),), -0.2, 0.2), 0.099609375, 1.0).astype(jnp.bfloat16)
    centroids = noise(key_list[5], (P_SIZE, D), 0.7, 4.1875, ((0, 16), (1, 8)))
    codebook = noise(key_list[6], (SUBS, K, SD), 0.7, 4.2, ((0, 8),), jnp.float32)
    variance = jnp.clip(jnp.exp(math.log(4.0) - 2.0794415 * jax.random.uniform(key_list[7], (SUBS,), jnp.float32) ** shard_levels(key_list[7], (SUBS,), ((0, 8),), -0.2, 0.2)), 0.5, 4.0)
    return dict(vectors=vectors, owner_group_index=owner_group_index, local_posting_index=local_posting_index, slot_valid_mask=slot_valid_mask, slot_posting_weight=slot_posting_weight, centroids=centroids, codebook=codebook, variance=variance)


def expect(resid, words, spread, weight):
    cross = jnp.dot(resid, words.T, precision=lax.Precision.HIGHEST, preferred_element_type=jnp.float32)
    dist = jnp.sum(resid * resid, axis=1)[:, None] - 2.0 * cross + jnp.sum(words * words, axis=1)[None, :]
    score = -dist / (2.0 * spread)
    top_score = jnp.max(score, axis=1, keepdims=True)
    expval = jnp.exp(score - top_score)
    resp = expval / jnp.sum(expval, axis=1, keepdims=True)
    weighted = resp * weight[:, None]
    sums = jnp.dot(weighted.T, resid, precision=lax.Precision.HIGHEST, preferred_element_type=jnp.float32)
    counts = jnp.sum(weighted, axis=0)
    error = jnp.sum(resp * dist, axis=1)
    return sums, counts, error


def reference(vectors, owner_group_index, local_posting_index, slot_valid_mask, slot_posting_weight, centroids, codebook, variance):
    row_count, slots_per_row = owner_group_index.shape
    posting = (owner_group_index * PDEV + local_posting_index).astype(jnp.int32).reshape(-1)
    row_of = (jnp.arange(row_count * slots_per_row, dtype=jnp.int32) // slots_per_row).astype(jnp.int32)
    valid = slot_valid_mask.reshape(-1).astype(jnp.float32)
    weight = slot_posting_weight.astype(jnp.float32).reshape(-1) * valid

    def residual_of(index):
        start = (index * SD).astype(jnp.int32)
        part_x = lax.dynamic_slice_in_dim(vectors, start, SD, 1)[row_of]
        part_c = lax.dynamic_slice_in_dim(centroids, start, SD, 1)[posting]
        return part_x.astype(jnp.float32) - part_c.astype(jnp.float32)

    def one_sub(packet):
        index, book, spread = packet
        return expect(residual_of(index), book, spread, weight)

    words = codebook.astype(jnp.float32)
    errors = jnp.zeros((SUBS, row_count * slots_per_row), jnp.float32)
    for step in range(ITERS):
        sums, counts, errors = lax.map(one_sub, (jnp.arange(SUBS, dtype=jnp.int32), words, variance))
        words = (sums + words) / (counts[:, :, None] + 1.0)
    slot_quant_error = (jnp.sum(errors, axis=0) / D) * valid
    return words, slot_quant_error.reshape(row_count, slots_per_row)
```

```python
import functools
import math

import jax
import jax.numpy as jnp
from jax import lax
from jax.experimental import pallas as pl
from jax.experimental.pallas import tpu as pltpu
from jax.sharding import Mesh
from jax.sharding import PartitionSpec as P

LOG2E = math.log2(math.e)
F32 = jnp.float32
BF16 = jnp.bfloat16
NT = (((1,), (1,)), ((), ()))
NN = (((1,), (0,)), ((), ()))
WINDOW = 64
TILE = 512
CAP = 768


def dot(a, b, dims=NN):
    return lax.dot_general(a, b, dims, preferred_element_type=F32)


def iota(shape, dim):
    return lax.broadcasted_iota(jnp.int32, shape, dim)


def ones_where(cond):
    return jnp.where(cond, 1.0, 0.0).astype(BF16)


def params(mib=48):
    return pltpu.CompilerParams(vmem_limit_bytes=mib << 20)


VMEM = pl.BlockSpec(memory_space=pltpu.VMEM)
SMEM = pl.BlockSpec(memory_space=pltpu.SMEM)


def block_place(r):
    d = lax.shift_right_logical(r, 1)
    y = lax.shift_right_logical(d, 3) & 3
    q = lax.shift_right_logical(d, 5) * 8 + (d & 7)
    return y, q


def list_kernel(cap, me_ref, ids_ref, out_ref):
    ids = ids_ref[...]
    mine = lax.shift_right_arithmetic(ids, 13) == me_ref[0]
    local = ids & 8191
    lane = iota((256, 128), 1)
    y, q = block_place(iota((256, 128), 0))
    keep = (q & 3) == lax.shift_right_logical(lane, 5)
    fold = ones_where((iota((128, 128), 0) & 31) == (iota((128, 128), 1) & 31))
    yc, qc = block_place(iota((32, 256), 1))
    pick = ones_where(yc * 8 + lax.shift_right_logical(qc, 2) == iota((32, 256), 0))

    def rows(x):
        x = dot(jnp.where(mine, x, 0).astype(F32).astype(BF16), fold)
        return dot(pick, jnp.where(keep, x, 0.0).astype(BF16))

    has = rows(jnp.ones_like(local))
    high = rows(lax.shift_right_logical(local, 7))
    low = rows(local & 127)
    has16 = has.astype(BF16)
    before = ones_where(iota((128, 128), 0) < iota((128, 128), 1))
    total = dot(has16, jnp.ones((128, 128), BF16))
    i0, i1 = iota((32, 32), 0), iota((32, 32), 1)
    earlier = ones_where((i1 < i0) & (lax.shift_right_logical(i1, 3) == lax.shift_right_logical(i0, 3)))
    rank = dot(has16, before) + dot(earlier, total.astype(BF16))
    rank = jnp.where(has > 0.5, rank, -1.0)
    sub = iota((8, 128), 0)
    place = iota((cap, 128), 0).astype(F32)
    for quarter in range(4):
        lhs, rhs = [], []
        for i in range(quarter * 8, quarter * 8 + 8):
            h = jnp.broadcast_to(high[i : i + 1], (8, 128))
            lo = jnp.broadcast_to(low[i : i + 1], (8, 128))
            lhs.append(jnp.where(sub == 0, h, jnp.where(sub == 1, lo, 0.0)).astype(BF16))
            rhs.append(ones_where(place == rank[i : i + 1]))
        got = dot(jnp.concatenate(lhs, 1), jnp.concatenate(rhs, 1), NT)
        out_ref[quarter : quarter + 1, :] = (got[0:1] * 128.0 + got[1:2]).astype(jnp.int32)


def key_kernel(cap, me_ref, ids_ref, key_ref, base_ref):
    owner = lax.shift_right_arithmetic(ids_ref[...], 13)
    lane = iota((256, 128), 1)
    count = jnp.zeros((256, 128), F32)
    for p in range(16):
        n = jnp.sum(jnp.where(owner == p, 1.0, 0.0), axis=1, keepdims=True)
        count = jnp.where(lane == p, n, count)
    count = count.astype(BF16)
    y, q = block_place(iota((32, 256), 1))
    b = iota((32, 256), 0)
    here = y == me_ref[0]
    start = dot(ones_where(here & (q < b)), count)
    first = dot(ones_where(here & (q < (b & ~1))), count).astype(jnp.int32)
    base = jnp.minimum(first & ~15, cap - WINDOW)
    base_ref[...] = base
    shift = (start - base.astype(F32)).astype(BF16)
    spread = ones_where(lax.shift_right_logical(iota((128, 1024), 1), 6) == iota((128, 1024), 0))
    gap = dot(shift, spread)
    col = iota((32, 1024), 1)
    key_ref[...] = jnp.where((col & 63).astype(F32) >= gap, col.astype(F32) - gap, -1.0)


def select_kernel(base_ref, key_ref, rows_ref, list_ref, out_ref):
    g = pl.program_id(0)
    parts = []
    for p in range(16):
        at = pl.multiple_of(base_ref[2 * g, p], 16)
        parts.append(list_ref[p, pl.ds(at, WINDOW), :])
    window = jnp.concatenate(parts, 0)
    meta = rows_ref[...].astype(F32)
    key = key_ref[0]
    hot = []
    for t in range(8):
        want = meta[:, t : t + 1] * 64.0 + meta[:, 8 + t : 9 + t]
        hot.append(ones_where(want[0:32] == key[0:1]))
        hot.append(ones_where(want[32:64] == key[1:2]))
    got = dot(jnp.concatenate(hot, 0), window).astype(BF16)
    for t in range(8):
        out_ref[t] = got[64 * t : 64 * t + 64]


def combine(parts, words):
    p0, p1, p2, p3 = parts
    total = (p0[...] + p2[...]) + (p1[...] + p3[...])

    def column(a):
        row = jnp.concatenate([total[256 + 2 * a : 257 + 2 * a], total[257 + 2 * a : 258 + 2 * a]], 1)
        return jnp.broadcast_to(row, (128, 256)).T

    count = jnp.where(iota((256, 128), 1) < 64, column(0), column(1))
    return (total[0:256] + words) / (count + 1.0)


def em_kernel(last, *refs):
    if last:
        p0, p1, p2, p3, rows_ref, cent_ref, words_ref, var_ref, out_ref, new_ref, err_ref = refs[:11]
        words = combine((p0, p1, p2, p3), words_ref[...])
        new_ref[...] = words
    else:
        rows_ref, cent_ref, words_ref, var_ref, out_ref = refs[:5]
        words = words_ref[...]
    mat_ref, weight_ref, acc_ref, count_ref = refs[-4:]
    scale = LOG2E / var_ref[...]
    scaled = words * scale
    left = iota((256, 128), 1) < 64
    biases = []
    for a in range(2):
        on = left if a == 0 else jnp.logical_not(left)
        x = jnp.where(on, scaled, 0.0)
        hi = x.astype(BF16).astype(F32)
        lo = x - hi
        mat_ref[a, :, 0:128] = hi.astype(BF16)
        mat_ref[a, :, 128:256] = (-hi).astype(BF16)
        mat_ref[a, :, 256:384] = lo.astype(BF16)
        mat_ref[a, :, 384:512] = (-lo).astype(BF16)
        biases.append(0.5 * jnp.sum(x * words, axis=1, keepdims=True))
    for c in range(8):
        flipped = rows_ref[128 * c : 128 * c + 128, 128:256].astype(F32).T
        weight_ref[:, 128 * c : 128 * c + 128] = flipped[16:24]
    acc_ref[...] = jnp.zeros_like(acc_ref)
    count_ref[...] = jnp.zeros_like(count_ref)

    def slots(t, carry):
        for c in range(1024 // TILE):
            at = pl.ds(c * TILE, TILE)
            v = rows_ref[at, 0:128]
            cent = cent_ref[t, at, :]
            x = jnp.concatenate([v, cent], 1)
            xx = jnp.concatenate([x, x], 1)
            tall = jnp.concatenate([x, x], 0)
            weight = weight_ref[pl.ds(t, 1), at]
            if last:
                r = v.astype(F32) - cent.astype(F32)
                r2 = r * r
                hi = r2.astype(BF16)
                lo = (r2 - hi.astype(F32)).astype(BF16)
                error = dot(jnp.ones((8, 256), BF16), jnp.concatenate([hi, lo], 1), NT)[0:1]
            for a in range(2):
                s = dot(mat_ref[a], xx, NT) - biases[a]
                top = jnp.max(s, axis=0, keepdims=True)
                e = jnp.exp2(s - top)
                inv = 1.0 / jnp.sum(e, axis=0, keepdims=True)
                if last:
                    mean = jnp.sum(e * s, axis=0, keepdims=True) * inv
                    error = error - mean * (2.0 / scale[0:1, 64 * a : 64 * a + 1])
                w = e * (inv * weight)
                w_hi = w.astype(BF16)
                w_lo = (w - w_hi.astype(F32)).astype(BF16)
                acc_ref[a] += dot(jnp.concatenate([w_hi, w_lo], 1), tall)
                n = w[:, 0:128]
                for k in range(1, TILE // 128):
                    n = n + w[:, 128 * k : 128 * k + 128]
                count_ref[a] += n
            if last:
                err_ref[pl.ds(t, 1), at] = error
        return carry

    lax.fori_loop(0, 8, slots, 0)
    diff = [acc_ref[a, :, 0:128] - acc_ref[a, :, 128:256] for a in range(2)]
    out_ref[0:256] = jnp.where(left, diff[0], diff[1])
    tail = []
    for a in range(2):
        row = jnp.sum(count_ref[a].T, axis=0, keepdims=True)
        tail += [row[:, 0:128], row[:, 128:256]]
    tail.append(jnp.zeros((4, 128), F32))
    out_ref[256:264] = jnp.concatenate(tail, 0)


def em(last, args):
    shapes = [jax.ShapeDtypeStruct((264, 128), F32)]
    if last:
        shapes += [jax.ShapeDtypeStruct((256, 128), F32), jax.ShapeDtypeStruct((8, 1024), F32)]
    return pl.pallas_call(
        functools.partial(em_kernel, last),
        out_shape=shapes,
        in_specs=[VMEM] * len(args),
        out_specs=[VMEM] * len(shapes),
        scratch_shapes=[
            pltpu.VMEM((2, 256, 512), BF16),
            pltpu.VMEM((8, 1024), F32),
            pltpu.VMEM((2, 256, 256), F32),
            pltpu.VMEM((2, 256, 128), F32),
        ],
        compiler_params=params(),
        name="em_last" if last else "em_first",
    )(*args)


def update_kernel(p0, p1, p2, p3, words_ref, out_ref):
    out_ref[...] = combine((p0, p1, p2, p3), words_ref[...])


def assemble_kernel(z_ref, x0, x1, x2, x3, out_ref):
    for d, x in enumerate((x0, x1, x2, x3)):
        at = 2 * ((z_ref[0] + (4 - d)) & 3)
        out_ref[at] = x[:, 0:64]
        out_ref[at + 1] = x[:, 64:128]


def shifts(x, axis):
    return [x] + [lax.ppermute(x, axis, [(i, (i + d) % 4) for i in range(4)]) for d in (1, 2, 3)]


def per_device(vectors, owner, local, mask, slot_weight, centroids, codebook, variance):
    z, y = lax.axis_index("z"), lax.axis_index("y")
    me = (z * 4 + y).astype(jnp.int32).reshape(1)
    y1, z1 = y.astype(jnp.int32).reshape(1), z.astype(jnp.int32).reshape(1)
    valid = mask > 0
    owned = jnp.where(valid, owner, -1)

    posting = jnp.where(valid, owner * 8192 + local, -1).T.reshape(1, 2, 128)
    ids = lax.all_to_all(
        jnp.broadcast_to(posting, (128, 2, 128)), ("z", "y", "sub"), 0, 0, tiled=True
    ).reshape(256, 128)

    wanted = pl.pallas_call(
        functools.partial(list_kernel, CAP),
        out_shape=jax.ShapeDtypeStruct((4, CAP), jnp.int32),
        in_specs=[SMEM, VMEM],
        out_specs=VMEM,
        compiler_params=params(),
        name="lists",
    )(me, ids)
    found = centroids.at[wanted.reshape(4 * CAP)].get(mode="promise_in_bounds")
    found = found.reshape(4, CAP, 4, 128).transpose(2, 0, 1, 3).reshape(16, CAP, 128)
    lists = lax.all_to_all(found, ("z", "y"), 0, 0, tiled=True)

    names = jnp.any(owned[:, :, None] == jnp.arange(16)[None, None, :], axis=1)
    upto = jnp.dot(jnp.tril(jnp.ones((32, 32), F32), -1), names.astype(F32))
    rank = jnp.sum(jnp.where(owned[:, :, None] == jnp.arange(16)[None, None, :], upto[:, None, :], 0.0), axis=2)
    weight = slot_weight * mask.astype(slot_weight.dtype)
    meta = jnp.concatenate([owned.astype(BF16), rank.astype(BF16), weight, jnp.zeros((32, 104), BF16)], 1)
    packed = jnp.concatenate(
        [
            vectors.reshape(32, 8, 4, 128).transpose(2, 1, 0, 3).reshape(32, 32, 128),
            jnp.broadcast_to(meta, (32, 32, 128)),
        ],
        2,
    )
    rows = lax.all_to_all(packed, ("z", "sub"), 0, 0, tiled=True).reshape(1024, 256)

    keys, base = pl.pallas_call(
        functools.partial(key_kernel, CAP),
        out_shape=(jax.ShapeDtypeStruct((32, 1024), F32), jax.ShapeDtypeStruct((32, 128), jnp.int32)),
        in_specs=[SMEM, VMEM],
        out_specs=(VMEM, VMEM),
        compiler_params=params(),
        name="keys",
    )(y1, ids)

    cents = pl.pallas_call(
        select_kernel,
        out_shape=jax.ShapeDtypeStruct((8, 1024, 128), BF16),
        grid_spec=pltpu.PrefetchScalarGridSpec(
            num_scalar_prefetch=1,
            grid=(16,),
            in_specs=[
                pl.BlockSpec((1, 2, 1024), lambda g, b: (g, 0, 0)),
                pl.BlockSpec((64, 128), lambda g, b: (g, 1)),
                pl.BlockSpec((16, CAP, 128), lambda g, b: (0, 0, 0)),
            ],
            out_specs=pl.BlockSpec((8, 64, 128), lambda g, b: (0, g, 0)),
        ),
        compiler_params=params(),
        name="select",
    )(base, keys.reshape(16, 2, 1024), rows, lists)

    words = lax.dynamic_slice(codebook, (2 * z, 0, 0), (2, 256, 64)).transpose(1, 0, 2).reshape(256, 128)
    spread = jnp.repeat(lax.dynamic_slice(variance, (2 * z,), (2,)), 64).reshape(1, 128)
    (part,) = em(False, (rows, cents, words, spread))
    part, words, error = em(True, (*shifts(part, "y"), rows, cents, words, spread))
    words = pl.pallas_call(
        update_kernel,
        out_shape=jax.ShapeDtypeStruct((256, 128), F32),
        in_specs=[VMEM] * 5,
        out_specs=VMEM,
        name="update",
    )(*shifts(part, "y"), words)
    trained = pl.pallas_call(
        assemble_kernel,
        out_shape=jax.ShapeDtypeStruct((8, 256, 64), F32),
        in_specs=[SMEM] + [VMEM] * 4,
        out_specs=VMEM,
        name="assemble",
    )(z1, *shifts(words, "z"))

    error = error.reshape(8, 32, 32).transpose(1, 0, 2)
    error = jnp.sum(lax.all_to_all(error, ("z", "sub"), 0, 0, tiled=True), axis=0).T
    return trained, error / vectors.shape[1] * mask.astype(F32)


def solution(mesh):
    grid = Mesh(mesh.devices.reshape(4, 4, 8), ("z", "y", "sub"))
    rows = P(("z", "y", "sub"), None)
    return jax.shard_map(
        per_device,
        mesh=grid,
        in_specs=(rows, rows, rows, rows, rows, P(("z", "y"), "sub"), P("sub", None, None), P("sub")),
        out_specs=(P("sub", None, None), rows),
        check_vma=False,
    )
```

```python
import functools
import math

import jax
import jax.numpy as jnp
from jax import lax
from jax.experimental import pallas as pl
from jax.experimental.pallas import tpu as pltpu
from jax.sharding import Mesh
from jax.sharding import PartitionSpec as P

LOG2E = math.log2(math.e)
F32 = jnp.float32
BF16 = jnp.bfloat16
NT = (((1,), (1,)), ((), ()))
NN = (((1,), (0,)), ((), ()))
WINDOW = 64
TILE = 512
CAP = 384


def dot(a, b, dims=NN):
    return lax.dot_general(a, b, dims, preferred_element_type=F32)


def iota(shape, dim):
    return lax.broadcasted_iota(jnp.int32, shape, dim)


def ones_where(cond):
    return jnp.where(cond, 1.0, 0.0).astype(BF16)


def params(mib=48):
    return pltpu.CompilerParams(vmem_limit_bytes=mib << 20)


VMEM = pl.BlockSpec(memory_space=pltpu.VMEM)
SMEM = pl.BlockSpec(memory_space=pltpu.SMEM)


def block_place(r):
    d = lax.shift_right_logical(r, 1)
    y = lax.shift_right_logical(d, 3) & 3
    q = lax.shift_right_logical(d, 5) * 8 + (d & 7)
    return y, q


def list_kernel(me_ref, ids_ref, first_ref, second_ref):
    ids = ids_ref[...]
    mine = lax.shift_right_arithmetic(ids, 13) == me_ref[0]
    local = ids & 8191
    lane = iota((256, 128), 1)
    _, q = block_place(iota((256, 128), 0))
    keep = (q & 3) == lax.shift_right_logical(lane, 5)
    fold = ones_where((iota((128, 128), 0) & 31) == (iota((128, 128), 1) & 31))
    yc, qc = block_place(iota((32, 256), 1))
    pick = ones_where(yc * 8 + lax.shift_right_logical(qc, 2) == iota((32, 256), 0))

    def rows(x):
        x = dot(jnp.where(mine, x, 0).astype(F32).astype(BF16), fold)
        return dot(pick, jnp.where(keep, x, 0.0).astype(BF16))

    has = rows(jnp.ones_like(local))
    high = rows(lax.shift_right_logical(local, 7))
    low = rows(local & 127)
    has16 = has.astype(BF16)
    before = ones_where(iota((128, 128), 0) < iota((128, 128), 1))
    total = dot(has16, jnp.ones((128, 128), BF16))
    i0, i1 = iota((32, 32), 0), iota((32, 32), 1)
    earlier = ones_where((i1 < i0) & (lax.shift_right_logical(i1, 2) == lax.shift_right_logical(i0, 2)))
    rank = dot(has16, before) + dot(earlier, total.astype(BF16))
    rank = jnp.where(has > 0.5, rank, -1.0)
    sub = iota((8, 128), 0)
    place = iota((CAP, 128), 0).astype(F32)
    for group in range(8):
        lhs, rhs = [], []
        for i in range(group * 4, group * 4 + 4):
            h = jnp.broadcast_to(high[i : i + 1], (8, 128))
            lo = jnp.broadcast_to(low[i : i + 1], (8, 128))
            lhs.append(jnp.where(sub == 0, h, jnp.where(sub == 1, lo, 0.0)).astype(BF16))
            rhs.append(ones_where(place == rank[i : i + 1]))
        got = dot(jnp.concatenate(lhs, 1), jnp.concatenate(rhs, 1), NT)
        out_ref = (first_ref, second_ref)[group % 2]
        quarter = group // 2
        out_ref[quarter : quarter + 1, :] = (got[0:1] * 128.0 + got[1:2]).astype(jnp.int32)


def key_kernel(me_ref, ids_ref, key_ref, base_ref):
    owner = lax.shift_right_arithmetic(ids_ref[...], 13)
    lane = iota((256, 128), 1)
    count = jnp.zeros((256, 128), F32)
    for p in range(16):
        n = jnp.sum(jnp.where(owner == p, 1.0, 0.0), axis=1, keepdims=True)
        count = jnp.where(lane == p, n, count)
    count = count.astype(BF16)
    y, q = block_place(iota((32, 256), 1))
    b = iota((32, 256), 0)
    here = (y == me_ref[0]) & (lax.shift_right_logical(q, 4) == lax.shift_right_logical(b, 4))
    start = dot(ones_where(here & (q < b)), count)
    first = dot(ones_where(here & (q < (b & ~1))), count).astype(jnp.int32)
    base = jnp.minimum(first & ~15, CAP - WINDOW)
    base_ref[...] = base
    shift = (start - base.astype(F32)).astype(BF16)
    spread = ones_where(lax.shift_right_logical(iota((128, 1024), 1), 6) == iota((128, 1024), 0))
    gap = dot(shift, spread)
    col = iota((32, 1024), 1)
    key_ref[...] = jnp.where((col & 63).astype(F32) >= gap, col.astype(F32) - gap, -1.0)


def split_kernel(rows_ref, out_ref):
    for c in range(4):
        out_ref[c] = rows_ref[:, 128 * c : 128 * c + 128]


def select_kernel(half, base_ref, key_ref, rows_ref, list_ref, out_ref):
    g = pl.program_id(0) + 8 * half
    parts = []
    for p in range(16):
        at = pl.multiple_of(base_ref[2 * g, p], 16)
        parts.append(list_ref[p, pl.ds(at, WINDOW), :])
    window = jnp.concatenate(parts, 0)
    meta = rows_ref[:, 128:256].astype(F32)
    key = key_ref[0]
    hot = []
    for t in range(8):
        want = meta[:, t : t + 1] * 64.0 + meta[:, 8 + t : 9 + t]
        hot.append(ones_where(want[0:32] == key[0:1]))
        hot.append(ones_where(want[32:64] == key[1:2]))
    got = dot(jnp.concatenate(hot, 0), window)
    v = rows_ref[:, 0:128].astype(F32)
    v_roll = pltpu.roll(v, 64, 1)
    left = iota((64, 128), 1) < 64
    for t in range(8):
        c = got[64 * t : 64 * t + 64]
        out_ref[0, t] = jnp.where(left, v, pltpu.roll(c, 64, 1)).astype(BF16)
        out_ref[1, t] = jnp.where(left, v_roll, c).astype(BF16)


def combine(parts, words):
    p0, p1, p2, p3 = parts
    total = (p0[...] + p2[...]) + (p1[...] + p3[...])

    def column(a):
        row = jnp.concatenate([total[256 + 2 * a : 257 + 2 * a], total[257 + 2 * a : 258 + 2 * a]], 1)
        return jnp.broadcast_to(row, (128, 256)).T

    count = jnp.where(iota((256, 128), 1) < 64, column(0), column(1))
    return (total[0:256] + words) / (count + 1.0)


def em_kernel(halves, carried, last, *refs):
    refs = list(refs)
    parts = [refs.pop(0) for _ in range(4)] if last else None
    base_ref = refs.pop(0) if carried else None
    x_refs = [refs.pop(0) for _ in halves]
    rows_ref, words_ref, var_ref, out_ref = refs[:4]
    if last:
        new_ref, err_ref = refs[4:6]
        words = combine(parts, words_ref[...])
        new_ref[...] = words
    else:
        words = words_ref[...]
    mat_ref, weight_ref, acc_ref = refs[-3:]
    scale = LOG2E / var_ref[...]
    scaled = words * scale
    rolled = pltpu.roll(scaled, 64, 1)
    left = iota((256, 128), 1) < 64
    biases = []
    for a in range(2):
        x = jnp.where(left, scaled, -rolled) if a == 0 else jnp.where(left, rolled, -scaled)
        hi = x.astype(BF16)
        mat_ref[a, :, 0:128] = hi
        mat_ref[a, :, 128:256] = (x - hi.astype(F32)).astype(BF16)
        mine = left if a == 0 else jnp.logical_not(left)
        biases.append(0.5 * jnp.sum(jnp.where(mine, scaled * words, 0.0), axis=1, keepdims=True))
    for half in halves:
        for c in range(4 * half, 4 * half + 4):
            flipped = rows_ref[128 * c : 128 * c + 128, 128:256].astype(F32).T
            weight_ref[:, 128 * c : 128 * c + 128] = flipped[16:24]
    acc_ref[...] = jnp.zeros_like(acc_ref)
    ones = jnp.ones((TILE, 128), BF16)

    def slots(t, carry):
        for h, half in enumerate(halves):
            for c in range(512 // TILE):
                at = pl.ds(c * TILE, TILE)
                weight = weight_ref[pl.ds(t, 1), pl.ds(512 * half + c * TILE, TILE)]
                error = jnp.zeros((1, TILE), F32)
                for a in range(2):
                    x = x_refs[h][a, t, at, :]
                    s = dot(mat_ref[a], jnp.concatenate([x, x], 1), NT) - biases[a]
                    top = jnp.max(s, axis=0, keepdims=True)
                    e = jnp.exp2(s - top)
                    inv = 1.0 / jnp.sum(e, axis=0, keepdims=True)
                    if last:
                        xf = x.astype(F32)
                        d = xf - pltpu.roll(xf, 64, 1)
                        d2 = d * d
                        hi = d2.astype(BF16)
                        lo = (d2 - hi.astype(F32)).astype(BF16)
                        r2 = dot(jnp.full((8, 256), 0.5, BF16), jnp.concatenate([hi, lo], 1), NT)[0:1]
                        mean = jnp.sum(e * s, axis=0, keepdims=True) * inv
                        error = error + (r2 - mean * (2.0 / scale[0:1, 64 * a : 64 * a + 1]))
                    w = e * (inv * weight)
                    w_hi = w.astype(BF16)
                    w_lo = (w - w_hi.astype(F32)).astype(BF16)
                    tall = jnp.concatenate([x, ones], 1)
                    acc_ref[a] += dot(jnp.concatenate([w_hi, w_lo], 1), jnp.concatenate([tall, tall], 0))
                if last:
                    for i in range(TILE // 256):
                        zb = (512 * half + c * TILE) // 256 + i
                        err_ref[zb, pl.ds(t, 1), :] = error[:, 256 * i : 256 * i + 256]
        return carry

    lax.fori_loop(0, 8, slots, 0)
    diff = [acc_ref[a, :, 0:128] - pltpu.roll(acc_ref[a, :, 0:128], 64, 1) for a in range(2)]
    sums = jnp.where(left, diff[0], -diff[1])
    tail = []
    for a in range(2):
        row = acc_ref[a, :, 128:256].T[0:1]
        tail += [row[:, 0:128], row[:, 128:256]]
    tail = jnp.concatenate(tail + [jnp.zeros((4, 128), F32)], 0)
    if carried:
        sums = sums + base_ref[0:256]
        tail = tail + base_ref[256:264]
    out_ref[0:256] = sums
    out_ref[256:264] = tail


def em(halves, carried, last, args):
    shapes = [jax.ShapeDtypeStruct((264, 128), F32)]
    if last:
        shapes += [jax.ShapeDtypeStruct((256, 128), F32), jax.ShapeDtypeStruct((4, 8, 256), F32)]
    return pl.pallas_call(
        functools.partial(em_kernel, halves, carried, last),
        out_shape=shapes,
        in_specs=[VMEM] * len(args),
        out_specs=[VMEM] * len(shapes),
        scratch_shapes=[
            pltpu.VMEM((2, 256, 256), BF16),
            pltpu.VMEM((8, 1024), F32),
            pltpu.VMEM((2, 256, 256), F32),
        ],
        compiler_params=params(),
        name="em_last" if last else "em_first",
    )(*args)


def update_kernel(p0, p1, p2, p3, words_ref, out_ref):
    out_ref[...] = combine((p0, p1, p2, p3), words_ref[...]).T


def assemble_kernel(z_ref, x0, x1, x2, x3, out_ref):
    for d, x in enumerate((x0, x1, x2, x3)):
        out_ref[(z_ref[0] + (4 - d)) & 3] = x[...]


def shifts(x, axis):
    return [x] + [lax.ppermute(x, axis, [(i, (i + d) % 4) for i in range(4)]) for d in (1, 2, 3)]


def per_device(vectors, owner, local, mask, slot_weight, centroids, codebook, variance):
    z, y = lax.axis_index("z"), lax.axis_index("y")
    me = (z * 4 + y).astype(jnp.int32).reshape(1)
    y1, z1 = y.astype(jnp.int32).reshape(1), z.astype(jnp.int32).reshape(1)
    valid = mask > 0
    owned = jnp.where(valid, owner, -1)

    posting = jnp.where(valid, owner * 8192 + local, -1).T.reshape(1, 2, 128)
    ids = lax.all_to_all(
        jnp.broadcast_to(posting, (128, 2, 128)), ("z", "y", "sub"), 0, 0, tiled=True
    ).reshape(256, 128)

    wanted = pl.pallas_call(
        list_kernel,
        out_shape=[jax.ShapeDtypeStruct((4, CAP), jnp.int32)] * 2,
        in_specs=[SMEM, VMEM],
        out_specs=[VMEM] * 2,
        compiler_params=params(),
        name="lists",
    )(me, ids)

    def fetch(want):
        found = centroids.at[want.reshape(4 * CAP)].get(mode="promise_in_bounds")
        found = pl.pallas_call(
            split_kernel,
            out_shape=jax.ShapeDtypeStruct((4, 4 * CAP, 128), BF16),
            in_specs=[VMEM],
            out_specs=VMEM,
            compiler_params=params(),
            name="split",
        )(found)
        return lax.all_to_all(found.reshape(16, CAP, 128), ("z", "y"), 0, 0, tiled=True)

    lists = [fetch(want) for want in wanted]

    names = jnp.any(owned[:, :, None] == jnp.arange(16)[None, None, :], axis=1)
    upto = jnp.dot(jnp.tril(jnp.ones((32, 32), F32), -1), names.astype(F32))
    rank = jnp.sum(jnp.where(owned[:, :, None] == jnp.arange(16)[None, None, :], upto[:, None, :], 0.0), axis=2)
    weight = slot_weight * mask.astype(slot_weight.dtype)
    meta = jnp.concatenate([owned.astype(BF16), rank.astype(BF16), weight, jnp.zeros((32, 104), BF16)], 1)
    packed = jnp.concatenate(
        [
            vectors.reshape(32, 8, 4, 128).transpose(2, 1, 0, 3).reshape(32, 32, 128),
            jnp.broadcast_to(meta, (32, 32, 128)),
        ],
        2,
    )
    rows = lax.all_to_all(packed, ("z", "sub"), 0, 0, tiled=True).reshape(1024, 256)

    keys, base = pl.pallas_call(
        key_kernel,
        out_shape=(jax.ShapeDtypeStruct((32, 1024), F32), jax.ShapeDtypeStruct((32, 128), jnp.int32)),
        in_specs=[SMEM, VMEM],
        out_specs=(VMEM, VMEM),
        compiler_params=params(),
        name="keys",
    )(y1, ids)
    keys = keys.reshape(16, 2, 1024)

    def select(half):
        return pl.pallas_call(
            functools.partial(select_kernel, half),
            out_shape=jax.ShapeDtypeStruct((2, 8, 512, 128), BF16),
            grid_spec=pltpu.PrefetchScalarGridSpec(
                num_scalar_prefetch=1,
                grid=(8,),
                in_specs=[
                    pl.BlockSpec((1, 2, 1024), lambda g, b: (g + 8 * half, 0, 0)),
                    pl.BlockSpec((64, 256), lambda g, b: (g + 8 * half, 0)),
                    pl.BlockSpec((16, CAP, 128), lambda g, b: (0, 0, 0)),
                ],
                out_specs=pl.BlockSpec((2, 8, 64, 128), lambda g, b: (0, 0, g, 0)),
            ),
            compiler_params=params(),
            name="select",
        )(base, keys, rows, lists[half])

    words = lax.dynamic_slice(codebook, (2 * z, 0, 0), (2, 256, 64)).transpose(1, 0, 2).reshape(256, 128)
    spread = jnp.repeat(lax.dynamic_slice(variance, (2 * z,), (2,)), 64).reshape(1, 128)
    x = [select(0)]
    (part,) = em((0,), False, False, (x[0], rows, words, spread))
    x.append(select(1))
    (part,) = em((1,), True, False, (part, x[1], rows, words, spread))
    part, words, error = em((0, 1), False, True, (*shifts(part, "y"), *x, rows, words, spread))
    turned = pl.pallas_call(
        update_kernel,
        out_shape=jax.ShapeDtypeStruct((128, 256), F32),
        in_specs=[VMEM] * 5,
        out_specs=VMEM,
        name="update",
    )(*shifts(part, "y"), words)
    trained = pl.pallas_call(
        assemble_kernel,
        out_shape=jax.ShapeDtypeStruct((4, 128, 256), F32),
        in_specs=[SMEM] + [VMEM] * 4,
        out_specs=VMEM,
        name="assemble",
    )(z1, *shifts(turned, "z"))
    trained = trained.reshape(8, 64, 256).transpose(0, 2, 1)

    error = jnp.sum(lax.all_to_all(error, "z", 0, 0, tiled=True), axis=0)
    error, _ = lax.optimization_barrier((error, turned))
    error = error.reshape(8, 8, 32).transpose(1, 0, 2)
    error = jnp.sum(lax.all_to_all(error, "sub", 0, 0, tiled=True), axis=0).T
    return trained, error / vectors.shape[1] * mask.astype(F32)


def solution(mesh):
    grid = Mesh(mesh.devices.reshape(4, 4, 8), ("z", "y", "sub"))
    rows = P(("z", "y", "sub"), None)
    return jax.shard_map(
        per_device,
        mesh=grid,
        in_specs=(rows, rows, rows, rows, rows, P(("z", "y"), "sub"), P("sub", None, None), P("sub")),
        out_specs=(P("sub", None, None), rows),
        check_vma=False,
    )
```

```python
import functools
import math

import jax
import jax.numpy as jnp
from jax import lax
from jax.experimental import pallas as pl
from jax.experimental.pallas import tpu as pltpu
from jax.sharding import Mesh
from jax.sharding import PartitionSpec as P

LOG2E = math.log2(math.e)
F32 = jnp.float32
BF16 = jnp.bfloat16
NT = (((1,), (1,)), ((), ()))
NN = (((1,), (0,)), ((), ()))
WINDOW = 32
TILE = 1024
CAP = 384


def dot(a, b, dims=NN):
    return lax.dot_general(a, b, dims, preferred_element_type=F32)


def iota(shape, dim):
    return lax.broadcasted_iota(jnp.int32, shape, dim)


def ones_where(cond):
    return jnp.where(cond, 1.0, 0.0).astype(BF16)


def params(mib=48):
    return pltpu.CompilerParams(vmem_limit_bytes=mib << 20)


VMEM = pl.BlockSpec(memory_space=pltpu.VMEM)
SMEM = pl.BlockSpec(memory_space=pltpu.SMEM)


def block_place(r):
    d = lax.shift_right_logical(r, 1)
    y = lax.shift_right_logical(d, 3) & 3
    q = lax.shift_right_logical(d, 5) * 8 + (d & 7)
    return y, q


def list_kernel(me_ref, ids_ref, first_ref, second_ref):
    ids = ids_ref[...]
    mine = lax.shift_right_arithmetic(ids, 13) == me_ref[0]
    local = ids & 8191
    lane = iota((256, 128), 1)
    _, q = block_place(iota((256, 128), 0))
    keep = (q & 3) == lax.shift_right_logical(lane, 5)
    fold = ones_where((iota((128, 128), 0) & 31) == (iota((128, 128), 1) & 31))
    yc, qc = block_place(iota((32, 256), 1))
    pick = ones_where(yc * 8 + lax.shift_right_logical(qc, 2) == iota((32, 256), 0))

    def rows(x):
        x = dot(jnp.where(mine, x, 0).astype(F32).astype(BF16), fold)
        return dot(pick, jnp.where(keep, x, 0.0).astype(BF16))

    has = rows(jnp.ones_like(local))
    high = rows(lax.shift_right_logical(local, 7))
    low = rows(local & 127)
    has16 = has.astype(BF16)
    before = ones_where(iota((128, 128), 0) < iota((128, 128), 1))
    total = dot(has16, jnp.ones((128, 128), BF16))
    i0, i1 = iota((32, 32), 0), iota((32, 32), 1)
    earlier = ones_where((i1 < i0) & (lax.shift_right_logical(i1, 2) == lax.shift_right_logical(i0, 2)))
    rank = dot(has16, before) + dot(earlier, total.astype(BF16))
    rank = jnp.where(has > 0.5, rank, -1.0)
    sub = iota((8, 128), 0)
    place = iota((CAP, 128), 0).astype(F32)
    for group in range(8):
        lhs, rhs = [], []
        for i in range(group * 4, group * 4 + 4):
            h = jnp.broadcast_to(high[i : i + 1], (8, 128))
            lo = jnp.broadcast_to(low[i : i + 1], (8, 128))
            lhs.append(jnp.where(sub == 0, h, jnp.where(sub == 1, lo, 0.0)).astype(BF16))
            rhs.append(ones_where(place == rank[i : i + 1]))
        got = dot(jnp.concatenate(lhs, 1), jnp.concatenate(rhs, 1), NT)
        out_ref = (first_ref, second_ref)[group % 2]
        quarter = group // 2
        out_ref[quarter : quarter + 1, :] = (got[0:1] * 128.0 + got[1:2]).astype(jnp.int32)


def key_kernel(me_ref, ids_ref, key_ref, base_ref):
    owner = lax.shift_right_arithmetic(ids_ref[...], 13)
    lane = iota((256, 128), 1)
    count = jnp.zeros((256, 128), F32)
    for p in range(16):
        n = jnp.sum(jnp.where(owner == p, 1.0, 0.0), axis=1, keepdims=True)
        count = jnp.where(lane == p, n, count)
    count = count.astype(BF16)
    y, q = block_place(iota((32, 256), 1))
    b = iota((32, 256), 0)
    here = (y == me_ref[0]) & (lax.shift_right_logical(q, 4) == lax.shift_right_logical(b, 4))
    start = dot(ones_where(here & (q < b)), count)
    base = jnp.minimum(start.astype(jnp.int32) & ~7, CAP - WINDOW)
    base_ref[...] = base
    shift = (start - base.astype(F32)).astype(BF16)
    spread = ones_where(lax.shift_right_logical(iota((128, 512), 1), 5) == iota((128, 512), 0))
    gap = dot(shift, spread)
    col = iota((32, 512), 1)
    key_ref[...] = jnp.where((col & 31).astype(F32) >= gap, col.astype(F32) - gap, -1.0)


def split_kernel(rows_ref, out_ref):
    for c in range(4):
        out_ref[c] = rows_ref[:, 128 * c : 128 * c + 128]


def select_kernel(half, base_ref, key_ref, rows_ref, list_ref, out_ref):
    g = pl.program_id(0) + 8 * half
    meta = rows_ref[:, 128:256].astype(F32)
    v = rows_ref[:, 0:128].astype(F32)
    v_roll = pltpu.roll(v, 64, 1)
    left = iota((32, 128), 1) < 64
    for b in range(2):
        parts = []
        for p in range(16):
            at = pl.multiple_of(base_ref[2 * g + b, p], 8)
            parts.append(list_ref[p, pl.ds(at, WINDOW), :])
        key = key_ref[0, b : b + 1]
        own = slice(32 * b, 32 * b + 32)
        hot = []
        for t in range(8):
            want = meta[own, t : t + 1] * float(WINDOW) + meta[own, 8 + t : 9 + t]
            hot.append(ones_where(want == key))
        got = dot(jnp.concatenate(hot, 0), jnp.concatenate(parts, 0))
        for t in range(8):
            c = got[32 * t : 32 * t + 32]
            out_ref[0, t, own] = jnp.where(left, v[own], pltpu.roll(c, 64, 1)).astype(BF16)
            out_ref[1, t, own] = jnp.where(left, v_roll[own], c).astype(BF16)


def combine(parts, words):
    p0, p1, p2, p3 = parts
    total = (p0[...] + p2[...]) + (p1[...] + p3[...])

    def column(a):
        row = jnp.concatenate([total[256 + 2 * a : 257 + 2 * a], total[257 + 2 * a : 258 + 2 * a]], 1)
        return jnp.broadcast_to(row, (128, 256)).T

    count = jnp.where(iota((256, 128), 1) < 64, column(0), column(1))
    return (total[0:256] + words) / (count + 1.0)


def em_kernel(halves, carried, last, *refs):
    refs = list(refs)
    parts = [refs.pop(0) for _ in range(4)] if last else None
    base_ref = refs.pop(0) if carried else None
    x_refs = [refs.pop(0) for _ in halves]
    rows_ref, words_ref, var_ref, out_ref = refs[:4]
    if last:
        new_ref, err_ref = refs[4:6]
        words = combine(parts, words_ref[...])
        new_ref[...] = words
    else:
        words = words_ref[...]
    mat_ref, weight_ref, acc_ref, slot_ref = refs[-4:]
    scale = LOG2E / var_ref[...]
    scaled = words * scale
    rolled = pltpu.roll(scaled, 64, 1)
    left = iota((256, 128), 1) < 64
    biases = []
    for a in range(2):
        x = jnp.where(left, scaled, -rolled) if a == 0 else jnp.where(left, rolled, -scaled)
        hi = x.astype(BF16)
        mat_ref[a, :, 0:128] = hi
        mat_ref[a, :, 128:256] = (x - hi.astype(F32)).astype(BF16)
        mine = left if a == 0 else jnp.logical_not(left)
        biases.append(0.5 * jnp.sum(jnp.where(mine, scaled * words, 0.0), axis=1, keepdims=True))
    for h, half in enumerate(halves):
        for c in range(4):
            flipped = rows_ref[512 * half + 128 * c : 512 * half + 128 * c + 128, 128:256].astype(F32).T
            for t in range(8):
                at = 512 * t + 128 * c
                weight_ref[h : h + 1, at : at + 128] = flipped[16 + t : 17 + t]
    acc_ref[...] = jnp.zeros_like(acc_ref)
    ones = jnp.ones((TILE, 128), BF16)

    def slots(i, carry):
        for h, half in enumerate(halves):
            at = pl.ds(pl.multiple_of(i * TILE, TILE), TILE)
            weight = weight_ref[h : h + 1, at]
            xs = [x_refs[h][a, at, :] for a in range(2)]
            if last:
                d2 = jnp.zeros((TILE, 128), F32)
                for x in xs:
                    d = x.astype(F32)
                    d = d - pltpu.roll(d, 64, 1)
                    d2 = d2 + d * d
                error = [jnp.sum(d2[128 * k : 128 * k + 128].T, axis=0, keepdims=True) for k in range(TILE // 128)]
                error = 0.5 * jnp.concatenate(error, 1)
            for a, x in enumerate(xs):
                s = dot(mat_ref[a], jnp.concatenate([x, x], 1), NT) - biases[a]
                top = jnp.max(s, axis=0, keepdims=True)
                e = jnp.exp2(s - top)
                inv = 1.0 / jnp.sum(e, axis=0, keepdims=True)
                if last:
                    mean = jnp.sum(e * s, axis=0, keepdims=True) * inv
                    error = error - mean * (2.0 / scale[0:1, 64 * a : 64 * a + 1])
                w = e * (inv * weight)
                w_hi = w.astype(BF16)
                w_lo = (w - w_hi.astype(F32)).astype(BF16)
                got = dot(jnp.concatenate([w_hi, w_lo], 0), jnp.concatenate([x, ones], 1))
                acc_ref[a] += got[0:256] + got[256:512]
            if last:
                for j in range(TILE // 512):
                    t = i * (TILE // 512) + j
                    slot_ref[pl.ds(t, 1), 512 * half : 512 * half + 512] = error[:, 512 * j : 512 * j + 512]
        return carry

    lax.fori_loop(0, 4096 // TILE, slots, 0)
    if last:
        for sd in range(8):
            pieces = [slot_ref[:, 32 * (8 * zd + sd) : 32 * (8 * zd + sd) + 32] for zd in range(4)]
            err_ref[sd] = jnp.concatenate(pieces, 1)
    diff = [acc_ref[a, :, 0:128] - pltpu.roll(acc_ref[a, :, 0:128], 64, 1) for a in range(2)]
    sums = jnp.where(left, diff[0], -diff[1])
    tail = []
    for a in range(2):
        row = acc_ref[a, :, 128:256].T[0:1]
        tail += [row[:, 0:128], row[:, 128:256]]
    tail = jnp.concatenate(tail + [jnp.zeros((4, 128), F32)], 0)
    if carried:
        sums = sums + base_ref[0:256]
        tail = tail + base_ref[256:264]
    out_ref[0:256] = sums
    out_ref[256:264] = tail


def em(halves, carried, last, args):
    shapes = [jax.ShapeDtypeStruct((264, 128), F32)]
    if last:
        shapes += [jax.ShapeDtypeStruct((256, 128), F32), jax.ShapeDtypeStruct((8, 8, 128), F32)]
    return pl.pallas_call(
        functools.partial(em_kernel, halves, carried, last),
        out_shape=shapes,
        in_specs=[VMEM] * len(args),
        out_specs=[VMEM] * len(shapes),
        scratch_shapes=[
            pltpu.VMEM((2, 256, 256), BF16),
            pltpu.VMEM((len(halves), 4096), F32),
            pltpu.VMEM((2, 256, 256), F32),
            pltpu.VMEM((8, 1024), F32),
        ],
        compiler_params=params(),
        name="em_last" if last else "em_first",
    )(*args)


def update_kernel(p0, p1, p2, p3, words_ref, err_ref, out_ref):
    out_ref[0:128] = combine((p0, p1, p2, p3), words_ref[...]).T
    total = err_ref[0]
    for s in range(1, 8):
        total = total + err_ref[s]
    out_ref[128:136] = jnp.concatenate([total, total], 1)


def assemble_kernel(z_ref, x0, x1, x2, x3, keep_ref, out_ref, err_ref):
    for d, x in enumerate((x0, x1, x2, x3)):
        out_ref[(z_ref[0] + (4 - d)) & 3] = x[0:128]
    error = (x0[128:136, 0:128] + x1[128:136, 0:128]) + (x2[128:136, 0:128] + x3[128:136, 0:128])
    error = pltpu.roll(error, (128 - 32 * z_ref[0]) & 127, 1)
    err_ref[...] = error[:, 0:32] * keep_ref[...]


def turn(d):
    return [(i, (i + d) % 4) for i in range(4)]


def shifts(x, axis):
    return [x] + [lax.ppermute(x, axis, turn(d)) for d in (1, 2, 3)]


def per_device(vectors, owner, local, mask, slot_weight, centroids, codebook, variance):
    z, y = lax.axis_index("z"), lax.axis_index("y")
    me = (z * 4 + y).astype(jnp.int32).reshape(1)
    y1, z1 = y.astype(jnp.int32).reshape(1), z.astype(jnp.int32).reshape(1)
    valid = mask > 0
    owned = jnp.where(valid, owner, -1)

    posting = jnp.where(valid, owner * 8192 + local, -1).T.reshape(1, 2, 128)
    ids = lax.all_to_all(
        jnp.broadcast_to(posting, (128, 2, 128)), ("z", "y", "sub"), 0, 0, tiled=True
    ).reshape(256, 128)

    wanted = pl.pallas_call(
        list_kernel,
        out_shape=[jax.ShapeDtypeStruct((4, CAP), jnp.int32)] * 2,
        in_specs=[SMEM, VMEM],
        out_specs=[VMEM] * 2,
        compiler_params=params(),
        name="lists",
    )(me, ids)

    def fetch(want):
        found = centroids.at[want.reshape(4 * CAP)].get(mode="promise_in_bounds")
        found = pl.pallas_call(
            split_kernel,
            out_shape=jax.ShapeDtypeStruct((4, 4 * CAP, 128), BF16),
            in_specs=[VMEM],
            out_specs=VMEM,
            compiler_params=params(),
            name="split",
        )(found)
        return lax.all_to_all(found.reshape(16, CAP, 128), ("z", "y"), 0, 0, tiled=True)

    lists = [fetch(want) for want in wanted]

    names = jnp.any(owned[:, :, None] == jnp.arange(16)[None, None, :], axis=1)
    upto = jnp.dot(jnp.tril(jnp.ones((32, 32), F32), -1), names.astype(F32))
    rank = jnp.sum(jnp.where(owned[:, :, None] == jnp.arange(16)[None, None, :], upto[:, None, :], 0.0), axis=2)
    weight = slot_weight * mask.astype(slot_weight.dtype)
    meta = jnp.concatenate([owned.astype(BF16), rank.astype(BF16), weight, jnp.zeros((32, 104), BF16)], 1)
    packed = jnp.concatenate(
        [
            vectors.reshape(32, 8, 4, 128).transpose(2, 1, 0, 3).reshape(32, 32, 128),
            jnp.broadcast_to(meta, (32, 32, 128)),
        ],
        2,
    )
    rows = lax.all_to_all(packed, ("z", "sub"), 0, 0, tiled=True).reshape(1024, 256)

    keys, base = pl.pallas_call(
        key_kernel,
        out_shape=(jax.ShapeDtypeStruct((32, 512), F32), jax.ShapeDtypeStruct((32, 128), jnp.int32)),
        in_specs=[SMEM, VMEM],
        out_specs=(VMEM, VMEM),
        compiler_params=params(),
        name="keys",
    )(y1, ids)
    keys = keys.reshape(16, 2, 512)

    def select(half):
        return pl.pallas_call(
            functools.partial(select_kernel, half),
            out_shape=jax.ShapeDtypeStruct((2, 8, 512, 128), BF16),
            grid_spec=pltpu.PrefetchScalarGridSpec(
                num_scalar_prefetch=1,
                grid=(8,),
                in_specs=[
                    pl.BlockSpec((1, 2, 512), lambda g, b: (g + 8 * half, 0, 0)),
                    pl.BlockSpec((64, 256), lambda g, b: (g + 8 * half, 0)),
                    pl.BlockSpec((16, CAP, 128), lambda g, b: (0, 0, 0)),
                ],
                out_specs=pl.BlockSpec((2, 8, 64, 128), lambda g, b: (0, 0, g, 0)),
            ),
            compiler_params=params(),
            name="select",
        )(base, keys, rows, lists[half]).reshape(2, 4096, 128)

    words = lax.dynamic_slice(codebook, (2 * z, 0, 0), (2, 256, 64)).transpose(1, 0, 2).reshape(256, 128)
    spread = jnp.repeat(lax.dynamic_slice(variance, (2 * z,), (2,)), 64).reshape(1, 128)
    x = [select(0)]
    (part,) = em((0,), False, False, (x[0], rows, words, spread))
    x.append(select(1))
    (part,) = em((1,), True, False, (part, x[1], rows, words, spread))
    part, words, error = em((0, 1), False, True, (*shifts(part, "y"), *x, rows, words, spread))
    error = lax.all_to_all(error, "sub", 0, 0, tiled=True)
    turned = pl.pallas_call(
        update_kernel,
        out_shape=jax.ShapeDtypeStruct((136, 256), F32),
        in_specs=[VMEM] * 6,
        out_specs=VMEM,
        name="update",
    )(*shifts(part, "y"), words, error)
    keep = mask.T.astype(F32) / vectors.shape[1]
    trained, error = pl.pallas_call(
        assemble_kernel,
        out_shape=[jax.ShapeDtypeStruct((4, 128, 256), F32), jax.ShapeDtypeStruct((8, 32), F32)],
        in_specs=[SMEM] + [VMEM] * 5,
        out_specs=[VMEM] * 2,
        name="assemble",
    )(z1, *shifts(turned, "z"), keep)
    return trained.reshape(8, 64, 256).transpose(0, 2, 1), error.T


def solution(mesh):
    grid = Mesh(mesh.devices.reshape(4, 4, 8), ("z", "y", "sub"))
    rows = P(("z", "y", "sub"), None)
    return jax.shard_map(
        per_device,
        mesh=grid,
        in_specs=(rows, rows, rows, rows, rows, P(("z", "y"), "sub"), P("sub", None, None), P("sub")),
        out_specs=(P("sub", None, None), rows),
        check_vma=False,
    )
```

```python
import functools
import math

import jax
import jax.numpy as jnp
from jax import lax
from jax.experimental import pallas as pl
from jax.experimental.pallas import tpu as pltpu
from jax.sharding import Mesh
from jax.sharding import PartitionSpec as P

LOG2E = math.log2(math.e)
F32 = jnp.float32
BF16 = jnp.bfloat16
NT = (((1,), (1,)), ((), ()))
NN = (((1,), (0,)), ((), ()))
WINDOW = 32
TILE = 1024
CAP = 384


def dot(a, b, dims=NN):
    return lax.dot_general(a, b, dims, preferred_element_type=F32)


def iota(shape, dim):
    return lax.broadcasted_iota(jnp.int32, shape, dim)


def ones_where(cond):
    return jnp.where(cond, 1.0, 0.0).astype(BF16)


def params(mib=8):
    return pltpu.CompilerParams(vmem_limit_bytes=mib << 20)


VMEM = pl.BlockSpec(memory_space=pltpu.VMEM)
SMEM = pl.BlockSpec(memory_space=pltpu.SMEM)


def block_place(r):
    d = lax.shift_right_logical(r, 1)
    y = lax.shift_right_logical(d, 3) & 3
    q = lax.shift_right_logical(d, 5) * 8 + (d & 7)
    return y, q


def send_kernel(owner_ref, local_ref, mask_ref, out_ref):
    posting = jnp.where(mask_ref[...] > 0, owner_ref[...] * 8192 + local_ref[...], -1)
    rows = [jnp.concatenate([posting[4 * h + t : 4 * h + t + 1] for t in range(4)], 1) for h in range(2)]
    out_ref[...] = jnp.broadcast_to(jnp.concatenate(rows, 0)[None], (128, 2, 128))


def list_kernel(me_ref, ids_ref, first_ref, second_ref):
    ids = ids_ref[...]
    mine = lax.shift_right_arithmetic(ids, 13) == me_ref[0]
    local = ids & 8191
    lane = iota((256, 128), 1)
    _, q = block_place(iota((256, 128), 0))
    keep = (q & 3) == lax.shift_right_logical(lane, 5)
    fold = ones_where((iota((128, 128), 0) & 31) == (iota((128, 128), 1) & 31))
    yc, qc = block_place(iota((32, 256), 1))
    pick = ones_where(yc * 8 + lax.shift_right_logical(qc, 2) == iota((32, 256), 0))

    def rows(x):
        x = dot(jnp.where(mine, x, 0).astype(F32).astype(BF16), fold)
        return dot(pick, jnp.where(keep, x, 0.0).astype(BF16))

    has = rows(jnp.ones_like(local))
    high = rows(lax.shift_right_logical(local, 7))
    low = rows(local & 127)
    has16 = has.astype(BF16)
    before = ones_where(iota((128, 128), 0) < iota((128, 128), 1))
    total = dot(has16, jnp.ones((128, 128), BF16))
    i0, i1 = iota((32, 32), 0), iota((32, 32), 1)
    earlier = ones_where((i1 < i0) & (lax.shift_right_logical(i1, 2) == lax.shift_right_logical(i0, 2)))
    rank = dot(has16, before) + dot(earlier, total.astype(BF16))
    rank = jnp.where(has > 0.5, rank, -1.0)
    sub = iota((8, 128), 0)
    place = iota((CAP, 128), 0).astype(F32)
    for group in range(8):
        lhs, rhs = [], []
        for i in range(group * 4, group * 4 + 4):
            h = jnp.broadcast_to(high[i : i + 1], (8, 128))
            lo = jnp.broadcast_to(low[i : i + 1], (8, 128))
            lhs.append(jnp.where(sub == 0, h, jnp.where(sub == 1, lo, 0.0)).astype(BF16))
            rhs.append(ones_where(place == rank[i : i + 1]))
        got = dot(jnp.concatenate(lhs, 1), jnp.concatenate(rhs, 1), NT)
        out_ref = (first_ref, second_ref)[group % 2]
        quarter = group // 2
        out_ref[quarter : quarter + 1, :] = (got[0:1] * 128.0 + got[1:2]).astype(jnp.int32)


def key_kernel(me_ref, ids_ref, key_ref, base_ref):
    owner = lax.shift_right_arithmetic(ids_ref[...], 13)
    lane = iota((256, 128), 1)
    count = jnp.zeros((256, 128), F32)
    for p in range(16):
        n = jnp.sum(jnp.where(owner == p, 1.0, 0.0), axis=1, keepdims=True)
        count = jnp.where(lane == p, n, count)
    count = count.astype(BF16)
    y, q = block_place(iota((32, 256), 1))
    b = iota((32, 256), 0)
    here = (y == me_ref[0]) & (lax.shift_right_logical(q, 4) == lax.shift_right_logical(b, 4))
    start = dot(ones_where(here & (q < b)), count)
    base = jnp.minimum(start.astype(jnp.int32) & ~7, CAP - WINDOW)
    base_ref[...] = base
    shift = (start - base.astype(F32)).astype(BF16)
    spread = ones_where(lax.shift_right_logical(iota((128, 512), 1), 5) == iota((128, 512), 0))
    gap = dot(shift, spread)
    col = iota((32, 512), 1)
    key_ref[...] = jnp.where((col & 31).astype(F32) >= gap, col.astype(F32) - gap, -1.0)


def split_kernel(rows_ref, out_ref, held_ref, sem):
    copies = []
    for c in range(4):
        held_ref[c] = rows_ref[:, 128 * c : 128 * c + 128]
        copies.append(pltpu.make_async_copy(held_ref.at[c], out_ref.at[c], sem.at[c]))
        copies[c].start()
    for copy in copies:
        copy.wait()


def select_kernel(half, base_ref, key_ref, rows_ref, list_ref, out_ref):
    left = iota((32, 128), 1) < 64

    def block(i):
        b = 16 * half + i
        rows = rows_ref[pl.ds(pl.multiple_of(32 * b, 32), 32), :].astype(F32)
        v, meta = rows[:, 0:128], rows[:, 128:256]
        v_roll = pltpu.roll(v, 64, 1)
        parts = []
        for p in range(16):
            at = pl.multiple_of(base_ref[b, p], 8)
            parts.append(list_ref[p, pl.ds(at, WINDOW), :])
        key = key_ref[pl.ds(b, 1), :]
        hot = []
        for t in range(8):
            want = meta[:, t : t + 1] * float(WINDOW) + meta[:, 8 + t : 9 + t]
            hot.append(ones_where(want == key))
        got = dot(jnp.concatenate(hot, 0), jnp.concatenate(parts, 0))
        own = pl.ds(pl.multiple_of(32 * i, 32), 32)
        for t in range(8):
            c = got[32 * t : 32 * t + 32]
            out_ref[0, t, own] = jnp.where(left, v, pltpu.roll(c, 64, 1)).astype(BF16)
            out_ref[1, t, own] = jnp.where(left, v_roll, c).astype(BF16)

    def pair(i, carry):
        block(2 * i)
        block(2 * i + 1)
        return carry

    lax.fori_loop(0, 8, pair, 0)


def combine(parts, words):
    p0, p1, p2, p3 = parts
    total = (p0[...] + p2[...]) + (p1[...] + p3[...])

    def column(a):
        row = jnp.concatenate([total[256 + 2 * a : 257 + 2 * a], total[257 + 2 * a : 258 + 2 * a]], 1)
        return jnp.broadcast_to(row, (128, 256)).T

    count = jnp.where(iota((256, 128), 1) < 64, column(0), column(1))
    return (total[0:256] + words) / (count + 1.0)


def em_kernel(halves, carried, last, *refs):
    refs = list(refs)
    parts = [refs.pop(0) for _ in range(4)] if last else None
    base_ref = refs.pop(0) if carried else None
    x_refs = [refs.pop(0) for _ in halves]
    rows_ref, words_ref, var_ref, out_ref = refs[:4]
    if last:
        new_ref, err_ref = refs[4:6]
        words = combine(parts, words_ref[...])
        new_ref[...] = words
    else:
        words = words_ref[...]
    mat_ref, weight_ref, acc_ref, slot_ref = refs[-4:]
    scale = LOG2E / var_ref[...]
    scaled = words * scale
    rolled = pltpu.roll(scaled, 64, 1)
    left = iota((256, 128), 1) < 64
    biases = []
    for a in range(2):
        x = jnp.where(left, scaled, -rolled) if a == 0 else jnp.where(left, rolled, -scaled)
        hi = x.astype(BF16)
        mat_ref[a, :, 0:128] = hi
        mat_ref[a, :, 128:256] = (x - hi.astype(F32)).astype(BF16)
        mine = left if a == 0 else jnp.logical_not(left)
        biases.append(0.5 * jnp.sum(jnp.where(mine, scaled * words, 0.0), axis=1, keepdims=True))
    for h, half in enumerate(halves):
        for c in range(4):
            flipped = rows_ref[512 * half + 128 * c : 512 * half + 128 * c + 128, 128:256].astype(F32).T
            for t in range(8):
                at = 512 * t + 128 * c
                weight_ref[h : h + 1, at : at + 128] = flipped[16 + t : 17 + t]
    acc_ref[...] = jnp.zeros_like(acc_ref)
    ones = jnp.ones((TILE, 128), BF16)

    def slots(i, carry):
        for h, half in enumerate(halves):
            at = pl.ds(pl.multiple_of(i * TILE, TILE), TILE)
            weight = weight_ref[h : h + 1, at]
            xs = [x_refs[h][a, at, :] for a in range(2)]
            if last:
                d2 = jnp.zeros((TILE, 128), F32)
                for x in xs:
                    d = x.astype(F32)
                    d = d - pltpu.roll(d, 64, 1)
                    d2 = d2 + d * d
                error = [jnp.sum(d2[128 * k : 128 * k + 128].T, axis=0, keepdims=True) for k in range(TILE // 128)]
                error = 0.5 * jnp.concatenate(error, 1)
            for a, x in enumerate(xs):
                s = dot(mat_ref[a], jnp.concatenate([x, x], 1), NT) - biases[a]
                top = jnp.max(s, axis=0, keepdims=True)
                e = jnp.exp2(s - top)
                inv = 1.0 / jnp.sum(e, axis=0, keepdims=True)
                if last:
                    mean = jnp.sum(e * s, axis=0, keepdims=True) * inv
                    error = error - mean * (2.0 / scale[0:1, 64 * a : 64 * a + 1])
                w = e * (inv * weight)
                w_hi = w.astype(BF16)
                w_lo = (w - w_hi.astype(F32)).astype(BF16)
                got = dot(jnp.concatenate([w_hi, w_lo], 0), jnp.concatenate([x, ones], 1))
                acc_ref[a] += got[0:256] + got[256:512]
            if last:
                for j in range(TILE // 512):
                    t = i * (TILE // 512) + j
                    slot_ref[pl.ds(t, 1), 512 * half : 512 * half + 512] = error[:, 512 * j : 512 * j + 512]
        return carry

    lax.fori_loop(0, 4096 // TILE, slots, 0)
    if last:
        for sd in range(8):
            pieces = [slot_ref[:, 32 * (8 * zd + sd) : 32 * (8 * zd + sd) + 32] for zd in range(4)]
            err_ref[sd] = jnp.concatenate(pieces, 1)
    diff = [acc_ref[a, :, 0:128] - pltpu.roll(acc_ref[a, :, 0:128], 64, 1) for a in range(2)]
    sums = jnp.where(left, diff[0], -diff[1])
    tail = []
    for a in range(2):
        row = acc_ref[a, :, 128:256].T[0:1]
        tail += [row[:, 0:128], row[:, 128:256]]
    tail = jnp.concatenate(tail + [jnp.zeros((4, 128), F32)], 0)
    if carried:
        sums = sums + base_ref[0:256]
        tail = tail + base_ref[256:264]
    out_ref[0:256] = sums
    out_ref[256:264] = tail


def em(halves, carried, last, args):
    shapes = [jax.ShapeDtypeStruct((264, 128), F32)]
    if last:
        shapes += [jax.ShapeDtypeStruct((256, 128), F32), jax.ShapeDtypeStruct((8, 8, 128), F32)]
    return pl.pallas_call(
        functools.partial(em_kernel, halves, carried, last),
        out_shape=shapes,
        in_specs=[VMEM] * len(args),
        out_specs=[VMEM] * len(shapes),
        scratch_shapes=[
            pltpu.VMEM((2, 256, 256), BF16),
            pltpu.VMEM((len(halves), 4096), F32),
            pltpu.VMEM((2, 256, 256), F32),
            pltpu.VMEM((8, 1024), F32),
        ],
        compiler_params=params(24),
        name="em_last" if last else "em_first",
    )(*args)


def update_kernel(p0, p1, p2, p3, words_ref, err_ref, out_ref):
    out_ref[0:128] = combine((p0, p1, p2, p3), words_ref[...]).T
    total = err_ref[0]
    for s in range(1, 8):
        total = total + err_ref[s]
    out_ref[128:136] = jnp.concatenate([total, total], 1)


def assemble_kernel(z_ref, x0, x1, x2, x3, keep_ref, out_ref, err_ref):
    for d, x in enumerate((x0, x1, x2, x3)):
        out_ref[(z_ref[0] + (4 - d)) & 3] = x[0:128]
    error = (x0[128:136, 0:128] + x1[128:136, 0:128]) + (x2[128:136, 0:128] + x3[128:136, 0:128])
    error = pltpu.roll(error, (128 - 32 * z_ref[0]) & 127, 1)
    err_ref[...] = error[:, 0:32] * keep_ref[...]


def turn(d):
    return [(i, (i + d) % 4) for i in range(4)]


def shifts(x, axis):
    return [x] + [lax.ppermute(x, axis, turn(d)) for d in (1, 2, 3)]


def per_device(vectors, owner, local, mask, slot_weight, centroids, codebook, variance):
    z, y = lax.axis_index("z"), lax.axis_index("y")
    me = (z * 4 + y).astype(jnp.int32).reshape(1)
    y1, z1 = y.astype(jnp.int32).reshape(1), z.astype(jnp.int32).reshape(1)
    valid = mask > 0
    owned = jnp.where(valid, owner, -1)

    posting = pl.pallas_call(
        send_kernel,
        out_shape=jax.ShapeDtypeStruct((128, 2, 128), jnp.int32),
        in_specs=[VMEM] * 3,
        out_specs=VMEM,
        name="send",
    )(owner.T, local.T, mask.T)
    ids = lax.all_to_all(posting, ("z", "y", "sub"), 0, 0, tiled=True).reshape(256, 128)

    wanted = pl.pallas_call(
        list_kernel,
        out_shape=[jax.ShapeDtypeStruct((4, CAP), jnp.int32)] * 2,
        in_specs=[SMEM, VMEM],
        out_specs=[VMEM] * 2,
        compiler_params=params(),
        name="lists",
    )(me, ids)

    def fetch(want):
        found = centroids.at[want.reshape(4 * CAP)].get(mode="promise_in_bounds")
        found = pl.pallas_call(
            split_kernel,
            out_shape=jax.ShapeDtypeStruct((4, 4 * CAP, 128), BF16),
            in_specs=[VMEM],
            out_specs=pl.BlockSpec(memory_space=pltpu.HBM),
            scratch_shapes=[pltpu.VMEM((4, 4 * CAP, 128), BF16), pltpu.SemaphoreType.DMA((4,))],
            compiler_params=params(),
            name="split",
        )(found)
        return lax.all_to_all(found.reshape(16, CAP, 128), ("z", "y"), 0, 0, tiled=True)

    lists = [fetch(want) for want in wanted]

    names = jnp.any(owned[:, :, None] == jnp.arange(16)[None, None, :], axis=1)
    upto = jnp.dot(jnp.tril(jnp.ones((32, 32), F32), -1), names.astype(F32))
    rank = jnp.sum(jnp.where(owned[:, :, None] == jnp.arange(16)[None, None, :], upto[:, None, :], 0.0), axis=2)
    weight = slot_weight * mask.astype(slot_weight.dtype)
    meta = jnp.concatenate([owned.astype(BF16), rank.astype(BF16), weight, jnp.zeros((32, 104), BF16)], 1)
    packed = jnp.concatenate(
        [
            vectors.reshape(32, 8, 4, 128).transpose(2, 1, 0, 3).reshape(32, 32, 128),
            jnp.broadcast_to(meta, (32, 32, 128)),
        ],
        2,
    )
    rows = lax.all_to_all(packed, ("z", "sub"), 0, 0, tiled=True).reshape(1024, 256)

    keys, base = pl.pallas_call(
        key_kernel,
        out_shape=(jax.ShapeDtypeStruct((32, 512), F32), jax.ShapeDtypeStruct((32, 128), jnp.int32)),
        in_specs=[SMEM, VMEM],
        out_specs=(VMEM, VMEM),
        compiler_params=params(),
        name="keys",
    )(y1, ids)

    def select(half):
        return pl.pallas_call(
            functools.partial(select_kernel, half),
            out_shape=jax.ShapeDtypeStruct((2, 8, 512, 128), BF16),
            in_specs=[SMEM] + [VMEM] * 3,
            out_specs=VMEM,
            compiler_params=params(12),
            name="select",
        )(base, keys, rows, lists[half]).reshape(2, 4096, 128)

    words = lax.dynamic_slice(codebook, (2 * z, 0, 0), (2, 256, 64)).transpose(1, 0, 2).reshape(256, 128)
    spread = jnp.repeat(lax.dynamic_slice(variance, (2 * z,), (2,)), 64).reshape(1, 128)
    x = [select(0)]
    (part,) = em((0,), False, False, (x[0], rows, words, spread))
    x.append(select(1))
    (part,) = em((1,), True, False, (part, x[1], rows, words, spread))
    part, words, error = em((0, 1), False, True, (*shifts(part, "y"), *x, rows, words, spread))
    error = lax.all_to_all(error, "sub", 0, 0, tiled=True)
    turned = pl.pallas_call(
        update_kernel,
        out_shape=jax.ShapeDtypeStruct((136, 256), F32),
        in_specs=[VMEM] * 6,
        out_specs=VMEM,
        compiler_params=params(),
        name="update",
    )(*shifts(part, "y"), words, error)
    keep = mask.T.astype(F32) / vectors.shape[1]
    trained, error = pl.pallas_call(
        assemble_kernel,
        out_shape=[jax.ShapeDtypeStruct((4, 128, 256), F32), jax.ShapeDtypeStruct((8, 32), F32)],
        in_specs=[SMEM] + [VMEM] * 5,
        out_specs=[VMEM] * 2,
        compiler_params=params(),
        name="assemble",
    )(z1, *shifts(turned, "z"), keep)
    return trained.reshape(8, 64, 256).transpose(0, 2, 1), error.T


def solution(mesh):
    grid = Mesh(mesh.devices.reshape(4, 4, 8), ("z", "y", "sub"))
    rows = P(("z", "y", "sub"), None)
    return jax.shard_map(
        per_device,
        mesh=grid,
        in_specs=(rows, rows, rows, rows, rows, P(("z", "y"), "sub"), P("sub", None, None), P("sub")),
        out_specs=(P("sub", None, None), rows),
        check_vma=False,
    )
```

```python
import functools
import math

import jax
import jax.numpy as jnp
from jax import lax
from jax.experimental import pallas as pl
from jax.experimental.pallas import tpu as pltpu
from jax.sharding import Mesh
from jax.sharding import PartitionSpec as P

LOG2E = math.log2(math.e)
F32 = jnp.float32
BF16 = jnp.bfloat16
NT = (((1,), (1,)), ((), ()))
NN = (((1,), (0,)), ((), ()))
WINDOW = 32
TILE = 2048
CAP = 384


def dot(a, b, dims=NN):
    return lax.dot_general(a, b, dims, preferred_element_type=F32)


def iota(shape, dim):
    return lax.broadcasted_iota(jnp.int32, shape, dim)


def ones_where(cond):
    return jnp.where(cond, 1.0, 0.0).astype(BF16)


def params(mib=8):
    return pltpu.CompilerParams(vmem_limit_bytes=mib << 20)


VMEM = pl.BlockSpec(memory_space=pltpu.VMEM)
SMEM = pl.BlockSpec(memory_space=pltpu.SMEM)


def block_place(r):
    d = lax.shift_right_logical(r, 1)
    y = lax.shift_right_logical(d, 3) & 3
    q = lax.shift_right_logical(d, 5) * 8 + (d & 7)
    return y, q


def send_kernel(owner_ref, local_ref, mask_ref, out_ref):
    posting = jnp.where(mask_ref[...] > 0, owner_ref[...] * 8192 + local_ref[...], -1)
    rows = [jnp.concatenate([posting[4 * h + t : 4 * h + t + 1] for t in range(4)], 1) for h in range(2)]
    out_ref[...] = jnp.broadcast_to(jnp.concatenate(rows, 0)[None], (128, 2, 128))


def list_kernel(me_ref, ids_ref, first_ref, second_ref):
    ids = ids_ref[...]
    mine = lax.shift_right_arithmetic(ids, 13) == me_ref[0]
    local = ids & 8191
    lane = iota((256, 128), 1)
    _, q = block_place(iota((256, 128), 0))
    keep = (q & 3) == lax.shift_right_logical(lane, 5)
    fold = ones_where((iota((128, 128), 0) & 31) == (iota((128, 128), 1) & 31))
    yc, qc = block_place(iota((32, 256), 1))
    pick = ones_where(yc * 8 + lax.shift_right_logical(qc, 2) == iota((32, 256), 0))

    def rows(x):
        x = dot(jnp.where(mine, x, 0).astype(F32).astype(BF16), fold)
        return dot(pick, jnp.where(keep, x, 0.0).astype(BF16))

    has = rows(jnp.ones_like(local))
    high = rows(lax.shift_right_logical(local, 7))
    low = rows(local & 127)
    has16 = has.astype(BF16)
    before = ones_where(iota((128, 128), 0) < iota((128, 128), 1))
    total = dot(has16, jnp.ones((128, 128), BF16))
    i0, i1 = iota((32, 32), 0), iota((32, 32), 1)
    earlier = ones_where((i1 < i0) & (lax.shift_right_logical(i1, 2) == lax.shift_right_logical(i0, 2)))
    rank = dot(has16, before) + dot(earlier, total.astype(BF16))
    rank = jnp.where(has > 0.5, rank, -1.0)
    sub = iota((8, 128), 0)
    place = iota((CAP, 128), 0).astype(F32)
    for group in range(8):
        lhs, rhs = [], []
        for i in range(group * 4, group * 4 + 4):
            h = jnp.broadcast_to(high[i : i + 1], (8, 128))
            lo = jnp.broadcast_to(low[i : i + 1], (8, 128))
            lhs.append(jnp.where(sub == 0, h, jnp.where(sub == 1, lo, 0.0)).astype(BF16))
            rhs.append(ones_where(place == rank[i : i + 1]))
        got = dot(jnp.concatenate(lhs, 1), jnp.concatenate(rhs, 1), NT)
        out_ref = (first_ref, second_ref)[group % 2]
        quarter = group // 2
        out_ref[quarter : quarter + 1, :] = (got[0:1] * 128.0 + got[1:2]).astype(jnp.int32)


def key_kernel(me_ref, ids_ref, key_ref, base_ref):
    owner = lax.shift_right_arithmetic(ids_ref[...], 13)
    lane = iota((256, 128), 1)
    count = jnp.zeros((256, 128), F32)
    for p in range(16):
        n = jnp.sum(jnp.where(owner == p, 1.0, 0.0), axis=1, keepdims=True)
        count = jnp.where(lane == p, n, count)
    count = count.astype(BF16)
    y, q = block_place(iota((32, 256), 1))
    b = iota((32, 256), 0)
    here = (y == me_ref[0]) & (lax.shift_right_logical(q, 4) == lax.shift_right_logical(b, 4))
    start = dot(ones_where(here & (q < b)), count)
    base = jnp.minimum(start.astype(jnp.int32) & ~7, CAP - WINDOW)
    base_ref[...] = base
    shift = (start - base.astype(F32)).astype(BF16)
    spread = ones_where(lax.shift_right_logical(iota((128, 512), 1), 5) == iota((128, 512), 0))
    gap = dot(shift, spread)
    col = iota((32, 512), 1)
    key_ref[...] = jnp.where((col & 31).astype(F32) >= gap, col.astype(F32) - gap, -1.0)


def split_kernel(rows_ref, out_ref, held_ref, sem):
    copies = []
    for c in range(4):
        held_ref[c] = rows_ref[:, 128 * c : 128 * c + 128]
        copies.append(pltpu.make_async_copy(held_ref.at[c], out_ref.at[c], sem.at[c]))
        copies[c].start()
    for copy in copies:
        copy.wait()


def select_kernel(half, base_ref, key_ref, rows_ref, list_ref, out_ref):
    left = iota((32, 128), 1) < 64

    def block(i):
        b = 16 * half + i
        rows = rows_ref[pl.ds(pl.multiple_of(32 * b, 32), 32), :].astype(F32)
        v, meta = rows[:, 0:128], rows[:, 128:256]
        v_roll = pltpu.roll(v, 64, 1)
        parts = []
        for p in range(16):
            at = pl.multiple_of(base_ref[b, p], 8)
            parts.append(list_ref[p, pl.ds(at, WINDOW), :])
        key = key_ref[pl.ds(b, 1), :]
        hot = []
        for t in range(8):
            want = meta[:, t : t + 1] * float(WINDOW) + meta[:, 8 + t : 9 + t]
            hot.append(ones_where(want == key))
        got = dot(jnp.concatenate(hot, 0), jnp.concatenate(parts, 0))
        own = pl.ds(pl.multiple_of(32 * i, 32), 32)
        for t in range(8):
            c = got[32 * t : 32 * t + 32]
            out_ref[0, t, own] = jnp.where(left, v, pltpu.roll(c, 64, 1)).astype(BF16)
            out_ref[1, t, own] = jnp.where(left, v_roll, c).astype(BF16)

    def pair(i, carry):
        block(2 * i)
        block(2 * i + 1)
        return carry

    lax.fori_loop(0, 8, pair, 0)


def combine(parts, words):
    p0, p1, p2, p3 = parts
    total = (p0[...] + p2[...]) + (p1[...] + p3[...])

    def column(a):
        row = jnp.concatenate([total[256 + 2 * a : 257 + 2 * a], total[257 + 2 * a : 258 + 2 * a]], 1)
        return jnp.broadcast_to(row, (128, 256)).T

    count = jnp.where(iota((256, 128), 1) < 64, column(0), column(1))
    return (total[0:256] + words) / (count + 1.0)


def em_kernel(halves, carried, last, *refs):
    refs = list(refs)
    parts = [refs.pop(0) for _ in range(4)] if last else None
    base_ref = refs.pop(0) if carried else None
    x_refs = [refs.pop(0) for _ in halves]
    rows_ref, words_ref, var_ref, out_ref = refs[:4]
    if last:
        new_ref, err_ref = refs[4:6]
        words = combine(parts, words_ref[...])
        new_ref[...] = words
    else:
        words = words_ref[...]
    mat_ref, weight_ref, acc_ref, slot_ref = refs[-4:]
    scale = LOG2E / var_ref[...]
    scaled = words * scale
    rolled = pltpu.roll(scaled, 64, 1)
    left = iota((256, 128), 1) < 64
    biases = []
    for a in range(2):
        x = jnp.where(left, scaled, -rolled) if a == 0 else jnp.where(left, rolled, -scaled)
        hi = x.astype(BF16)
        mat_ref[a, :, 0:128] = hi
        mat_ref[a, :, 128:256] = (x - hi.astype(F32)).astype(BF16)
        mine = left if a == 0 else jnp.logical_not(left)
        biases.append(0.5 * jnp.sum(jnp.where(mine, scaled * words, 0.0), axis=1, keepdims=True))
    for h, half in enumerate(halves):
        for c in range(4):
            flipped = rows_ref[512 * half + 128 * c : 512 * half + 128 * c + 128, 128:256].astype(F32).T
            for t in range(8):
                at = 512 * t + 128 * c
                weight_ref[h : h + 1, at : at + 128] = flipped[16 + t : 17 + t]
    acc_ref[...] = jnp.zeros_like(acc_ref)
    ones = jnp.ones((TILE, 128), BF16)

    def slots(i, carry):
        for h, half in enumerate(halves):
            at = pl.ds(pl.multiple_of(i * TILE, TILE), TILE)
            weight = weight_ref[h : h + 1, at]
            xs = [x_refs[h][a, at, :] for a in range(2)]
            if last:
                d2 = jnp.zeros((TILE, 128), F32)
                for x in xs:
                    d = x.astype(F32)
                    d = d - pltpu.roll(d, 64, 1)
                    d2 = d2 + d * d
                error = [jnp.sum(d2[128 * k : 128 * k + 128].T, axis=0, keepdims=True) for k in range(TILE // 128)]
                error = 0.5 * jnp.concatenate(error, 1)
            for a, x in enumerate(xs):
                s = dot(mat_ref[a], jnp.concatenate([x, x], 1), NT) - biases[a]
                top = jnp.max(s, axis=0, keepdims=True)
                e = jnp.exp2(s - top)
                inv = 1.0 / jnp.sum(e, axis=0, keepdims=True)
                if last:
                    mean = jnp.sum(e * s, axis=0, keepdims=True) * inv
                    error = error - mean * (2.0 / scale[0:1, 64 * a : 64 * a + 1])
                w = e * (inv * weight)
                w_hi = w.astype(BF16)
                w_lo = (w - w_hi.astype(F32)).astype(BF16)
                got = dot(jnp.concatenate([w_hi, w_lo], 0), jnp.concatenate([x, ones], 1))
                acc_ref[a] += got[0:256] + got[256:512]
            if last:
                for j in range(TILE // 512):
                    t = i * (TILE // 512) + j
                    slot_ref[pl.ds(t, 1), 512 * half : 512 * half + 512] = error[:, 512 * j : 512 * j + 512]
        return carry

    lax.fori_loop(0, 4096 // TILE, slots, 0)
    if last:
        for sd in range(8):
            pieces = [slot_ref[:, 32 * (8 * zd + sd) : 32 * (8 * zd + sd) + 32] for zd in range(4)]
            err_ref[sd] = jnp.concatenate(pieces, 1)
    diff = [acc_ref[a, :, 0:128] - pltpu.roll(acc_ref[a, :, 0:128], 64, 1) for a in range(2)]
    sums = jnp.where(left, diff[0], -diff[1])
    tail = []
    for a in range(2):
        row = acc_ref[a, :, 128:256].T[0:1]
        tail += [row[:, 0:128], row[:, 128:256]]
    tail = jnp.concatenate(tail + [jnp.zeros((4, 128), F32)], 0)
    if carried:
        sums = sums + base_ref[0:256]
        tail = tail + base_ref[256:264]
    out_ref[0:256] = sums
    out_ref[256:264] = tail


def em(halves, carried, last, args):
    shapes = [jax.ShapeDtypeStruct((264, 128), F32)]
    if last:
        shapes += [jax.ShapeDtypeStruct((256, 128), F32), jax.ShapeDtypeStruct((8, 8, 128), F32)]
    return pl.pallas_call(
        functools.partial(em_kernel, halves, carried, last),
        out_shape=shapes,
        in_specs=[VMEM] * len(args),
        out_specs=[VMEM] * len(shapes),
        scratch_shapes=[
            pltpu.VMEM((2, 256, 256), BF16),
            pltpu.VMEM((len(halves), 4096), F32),
            pltpu.VMEM((2, 256, 256), F32),
            pltpu.VMEM((8, 1024), F32),
        ],
        compiler_params=params(24),
        name="em_last" if last else "em_first",
    )(*args)


def update_kernel(p0, p1, p2, p3, words_ref, err_ref, out_ref):
    out_ref[0:128] = combine((p0, p1, p2, p3), words_ref[...]).T
    total = err_ref[0]
    for s in range(1, 8):
        total = total + err_ref[s]
    out_ref[128:136] = jnp.concatenate([total, total], 1)


def assemble_kernel(z_ref, x0, x1, x2, x3, keep_ref, out_ref, err_ref):
    for d, x in enumerate((x0, x1, x2, x3)):
        out_ref[(z_ref[0] + (4 - d)) & 3] = x[0:128]
    error = (x0[128:136, 0:128] + x1[128:136, 0:128]) + (x2[128:136, 0:128] + x3[128:136, 0:128])
    error = pltpu.roll(error, (128 - 32 * z_ref[0]) & 127, 1)
    err_ref[...] = error[:, 0:32] * keep_ref[...]


def turn(d):
    return [(i, (i + d) % 4) for i in range(4)]


def shifts(x, axis):
    return [x] + [lax.ppermute(x, axis, turn(d)) for d in (1, 2, 3)]


def per_device(vectors, owner, local, mask, slot_weight, centroids, codebook, variance):
    z, y = lax.axis_index("z"), lax.axis_index("y")
    me = (z * 4 + y).astype(jnp.int32).reshape(1)
    y1, z1 = y.astype(jnp.int32).reshape(1), z.astype(jnp.int32).reshape(1)
    valid = mask > 0
    owned = jnp.where(valid, owner, -1)

    posting = pl.pallas_call(
        send_kernel,
        out_shape=jax.ShapeDtypeStruct((128, 2, 128), jnp.int32),
        in_specs=[VMEM] * 3,
        out_specs=VMEM,
        name="send",
    )(owner.T, local.T, mask.T)
    ids = lax.all_to_all(posting, ("z", "y", "sub"), 0, 0, tiled=True).reshape(256, 128)

    wanted = pl.pallas_call(
        list_kernel,
        out_shape=[jax.ShapeDtypeStruct((4, CAP), jnp.int32)] * 2,
        in_specs=[SMEM, VMEM],
        out_specs=[VMEM] * 2,
        compiler_params=params(),
        name="lists",
    )(me, ids)

    def fetch(want):
        found = centroids.at[want.reshape(4 * CAP)].get(mode="promise_in_bounds")
        found = pl.pallas_call(
            split_kernel,
            out_shape=jax.ShapeDtypeStruct((4, 4 * CAP, 128), BF16),
            in_specs=[VMEM],
            out_specs=pl.BlockSpec(memory_space=pltpu.HBM),
            scratch_shapes=[pltpu.VMEM((4, 4 * CAP, 128), BF16), pltpu.SemaphoreType.DMA((4,))],
            compiler_params=params(),
            name="split",
        )(found)
        return lax.all_to_all(found.reshape(16, CAP, 128), ("z", "y"), 0, 0, tiled=True)

    lists = [fetch(want) for want in wanted]

    names = jnp.any(owned[:, :, None] == jnp.arange(16)[None, None, :], axis=1)
    upto = jnp.dot(jnp.tril(jnp.ones((32, 32), F32), -1), names.astype(F32))
    rank = jnp.sum(jnp.where(owned[:, :, None] == jnp.arange(16)[None, None, :], upto[:, None, :], 0.0), axis=2)
    weight = slot_weight * mask.astype(slot_weight.dtype)
    meta = jnp.concatenate([owned.astype(BF16), rank.astype(BF16), weight, jnp.zeros((32, 104), BF16)], 1)
    packed = jnp.concatenate(
        [
            vectors.reshape(32, 8, 4, 128).transpose(2, 1, 0, 3).reshape(32, 32, 128),
            jnp.broadcast_to(meta, (32, 32, 128)),
        ],
        2,
    )
    rows = lax.all_to_all(packed, ("z", "sub"), 0, 0, tiled=True).reshape(1024, 256)

    keys, base = pl.pallas_call(
        key_kernel,
        out_shape=(jax.ShapeDtypeStruct((32, 512), F32), jax.ShapeDtypeStruct((32, 128), jnp.int32)),
        in_specs=[SMEM, VMEM],
        out_specs=(VMEM, VMEM),
        compiler_params=params(),
        name="keys",
    )(y1, ids)

    def select(half):
        return pl.pallas_call(
            functools.partial(select_kernel, half),
            out_shape=jax.ShapeDtypeStruct((2, 8, 512, 128), BF16),
            in_specs=[SMEM] + [VMEM] * 3,
            out_specs=VMEM,
            compiler_params=params(12),
            name="select",
        )(base, keys, rows, lists[half]).reshape(2, 4096, 128)

    words = lax.dynamic_slice(codebook, (2 * z, 0, 0), (2, 256, 64)).transpose(1, 0, 2).reshape(256, 128)
    spread = jnp.repeat(lax.dynamic_slice(variance, (2 * z,), (2,)), 64).reshape(1, 128)
    x = [select(0)]
    (part,) = em((0,), False, False, (x[0], rows, words, spread))
    x.append(select(1))
    (part,) = em((1,), True, False, (part, x[1], rows, words, spread))
    part, words, error = em((0, 1), False, True, (*shifts(part, "y"), *x, rows, words, spread))
    error = lax.all_to_all(error, "sub", 0, 0, tiled=True)
    turned = pl.pallas_call(
        update_kernel,
        out_shape=jax.ShapeDtypeStruct((136, 256), F32),
        in_specs=[VMEM] * 6,
        out_specs=VMEM,
        compiler_params=params(),
        name="update",
    )(*shifts(part, "y"), words, error)
    keep = mask.T.astype(F32) / vectors.shape[1]
    trained, error = pl.pallas_call(
        assemble_kernel,
        out_shape=[jax.ShapeDtypeStruct((4, 128, 256), F32), jax.ShapeDtypeStruct((8, 32), F32)],
        in_specs=[SMEM] + [VMEM] * 5,
        out_specs=[VMEM] * 2,
        compiler_params=params(),
        name="assemble",
    )(z1, *shifts(turned, "z"), keep)
    return trained.reshape(8, 64, 256).transpose(0, 2, 1), error.T


def solution(mesh):
    grid = Mesh(mesh.devices.reshape(4, 4, 8), ("z", "y", "sub"))
    rows = P(("z", "y", "sub"), None)
    return jax.shard_map(
        per_device,
        mesh=grid,
        in_specs=(rows, rows, rows, rows, rows, P(("z", "y"), "sub"), P("sub", None, None), P("sub")),
        out_specs=(P("sub", None, None), rows),
        check_vma=False,
    )
```
